32 devices in a mesh: space: 8 (over z, x), lag: 4 (over y, core).
Axes of the slice: x: 2, y: 2, z: 4, core: 2. Of those that a mesh axis runs over, the one named last changes fastest.
Arguments:
- ensemble: bfloat16 [8, 4096, 1024], P('lag', 'space'), may hold values from -6 to 6
- observed: float32 [2, 512, 1024], replicated, may hold values from -8 to 8
- obs_error: float32 [2, 512], replicated, may hold values from 0.1 to 1
- gauge_rows: int32 [2, 512], replicated, may hold values from 0 to 4095
Outputs:
- smoothed: bfloat16 [8, 4096, 1024], P('lag', 'space')
The draws below stay inside these ranges and needn't reach their ends.
All inputs are finite; a program needn't handle non-finite values.
Results may differ from the reference program's by a relative error of at most 0.0085.
Values sent between devices are 32-bit elements; how exact they have to be, the bound alone decides.
A program may use at most 64 MiB of HBM per device.

```python
import math
import jax
import jax.numpy as jnp
from jax import lax

MEMBERS = 1024
GAUGES = 512
STATE_ROWS = 4096
LAGS = 8


def place_ends(values, rng, low, top_value):
    dims = values.shape
    spot = [jax.random.randint(jax.random.fold_in(rng, axis), (), 0, dims[axis]) for axis in range(len(dims))]
    values = values.at[tuple(spot)].set(low)
    longest = dims.index(max(dims))
    spot[longest] = (spot[longest] + 1) % dims[longest]
    return values.at[tuple(spot)].set(top_value)


def levels(key, dims, pieces, low, largest):
    factor_of = 1.0
    for axis_at, parts in pieces:
        heights = jax.random.uniform(jax.random.fold_in(jax.random.fold_in(key, 6), axis_at), (parts,), jnp.float32, low / len(pieces), largest / len(pieces))
        factor_of = factor_of * jnp.repeat(jnp.exp(heights), dims[axis_at] // parts).reshape((-1,) + (1,) * (len(dims) - 1 - axis_at))
    return factor_of


def bell_draw(stream_key, extent, scale, most, cuts=(), held_as=jnp.bfloat16):
    array = scale * jax.random.normal(stream_key, extent, jnp.float32)
    if cuts:
        array = array * levels(stream_key, extent, cuts, -0.22, 0.18)
    return jnp.clip(array, -most, most).astype(held_as)


def setup_inputs(seed: int = 0) -> dict:
    key_of = jax.random.split(jax.random.key(seed), 5)
    ensemble = bell_draw(key_of[0], (LAGS, STATE_ROWS, MEMBERS), 1.0, 6.0, ((0, 4), (1, 8)))
    observed = bell_draw(key_of[1], (2, GAUGES, MEMBERS), 1.5, 8.0, (), jnp.float32)
    obs_error = jnp.clip(jnp.exp(jax.random.uniform(key_of[2], (2, GAUGES), jnp.float32, math.log(0.1), math.log(1.0))), 0.1, 1.0)
    gauge_rows = place_ends(jax.random.randint(key_of[3], (2, GAUGES), 0, STATE_ROWS), jax.random.fold_in(key_of[3], 1), 0, STATE_ROWS - 1).astype(jnp.int32)
    return {"ensemble": ensemble, "observed": observed, "obs_error": obs_error, "gauge_rows": gauge_rows}


def transform(hx_rows, observed_k, error_k):
    members = hx_rows.shape[1]
    anomaly = hx_rows - jnp.mean(hx_rows, axis=1, keepdims=True)
    innov = observed_k - hx_rows
    cov = jnp.dot(anomaly, anomaly.T, precision=lax.Precision.HIGHEST) / (members - 1.0)
    cov = cov + jnp.diag(error_k)
    factor = jnp.linalg.cholesky(cov)
    middle = lax.linalg.triangular_solve(factor, innov, left_side=True, lower=True, transpose_a=False)
    solved = lax.linalg.triangular_solve(factor, middle, left_side=True, lower=True, transpose_a=True)
    gain = jnp.dot(anomaly.T, solved, precision=lax.Precision.HIGHEST) / (members - 1.0)
    return jnp.eye(members, dtype=gain.dtype) + gain

def reference(ensemble, observed, obs_error, gauge_rows):
    newest = ensemble[-1].astype(jnp.float32)
    weights_one = transform(newest[gauge_rows[0]], observed[0], obs_error[0])

    def first_of(slab):
        return jnp.dot(slab.astype(jnp.float32), weights_one, precision=lax.Precision.HIGHEST)
    first = lax.map(first_of, ensemble)
    weights_two = transform(first[-1][gauge_rows[1]], observed[1], obs_error[1])

    def second_of(slab):
        return jnp.dot(slab, weights_two, precision=lax.Precision.HIGHEST).astype(jnp.bfloat16)
    return lax.map(second_of, first)
```

```python
import functools

import jax
import jax.numpy as jnp
from jax import lax
from jax.experimental import pallas as pl
from jax.experimental.pallas import tpu as pltpu
from jax.sharding import PartitionSpec as P

BF = jnp.bfloat16
F32 = jnp.float32
MESH = pl.DeviceIdType.MESH


def pad_even(n):
    return 2 if n % 2 == 0 else 1


def side(n):
    best = 1
    for inner in range(1, n + 1):
        if n % inner == 0 and inner * inner <= n:
            best = inner
    return best


def gather_kernel(nspace, nlag, p_ref, out_ref, acc, xin, zin, xs, xr, zs, zr, ys, ar):
    nx = side(nspace)
    nz = nspace // nx
    nc = pad_even(nlag)
    ny = nlag // nc
    chunk = p_ref.shape[1] // nspace
    s = lax.axis_index("space")
    l = lax.axis_index("lag")
    z, x = s // nx, s % nx
    y, core = l // nc, l % nc
    newest = l == nlag - 1
    relay = core == nc - 1

    def rows(t):
        return pl.ds(pl.multiple_of(t * chunk, chunk), chunk)

    def at(dz, dx):
        return lax.rem(z + dz, nz) * nx + lax.rem(x + dx, nx)

    def send(src, dst, send_sem, recv_sem, space, lag):
        return pltpu.make_async_remote_copy(
            src_ref=src, dst_ref=dst, send_sem=send_sem, recv_sem=recv_sem,
            device_id=(space, lag), device_id_type=MESH,
        )

    order = list(range(1, nz)) + [0]

    def x_copy(k, dz, dx):
        t = at(dz, dx)
        i = (k * nz + dz) * nx + dx
        return send(p_ref.at[k, rows(t)], xin.at[i], xs.at[i], xr.at[i], at(0, dx), l)

    def z_copy(k, dz):
        i = k * nz + dz
        return send(acc.at[i], zin.at[i], zs.at[i], zr.at[i], at(dz, 0), l)

    def out_copy(k, t, slot, space, lag):
        return send(
            out_ref.at[k, rows(t)], out_ref.at[k, rows(t)],
            ys.at[k, t, slot], ar.at[k, t], space, lag,
        )

    def arrived(k, t):
        pltpu.make_async_copy(
            out_ref.at[k, rows(t)], out_ref.at[k, rows(t)], ar.at[k, t]
        ).wait()

    base_c = nx - 1
    base_z = base_c + (nc - 1)
    base_y = base_z + (nz - 1)

    def own_targets(k):
        copies = [out_copy(k, s, base_z + dz - 1, at(dz, 0), l) for dz in range(nz - 1, 0, -1)]
        copies += [out_copy(k, s, dx - 1, at(0, dx), l) for dx in range(1, nx)]
        copies += [out_copy(k, s, base_c + c, s, y * nc + c) for c in range(nc - 1)]
        return copies

    def plane_targets(k):
        return [out_copy(k, s, base_y + p, s, p * nc + nc - 1) for p in range(ny - 1)]

    def z_targets(k, dz):
        t = at(dz, 0)
        copies = [out_copy(k, t, dx - 1, at(0, dx), l) for dx in range(1, nx)]
        return copies + [out_copy(k, t, base_c + c, s, y * nc + c) for c in range(nc - 1)]

    def x_targets(k, dz, dx):
        t = at(dz, dx)
        return [out_copy(k, t, base_c + c, s, y * nc + c) for c in range(nc - 1)]

    @pl.when(newest)
    def _():
        for k in range(2):
            for dz in order:
                for dx in range(1, nx):
                    x_copy(k, dz, dx).start()
        for k in range(2):
            for dz in order:
                total = p_ref[k, rows(at(dz, 0)), :]
                for dx in range(1, nx):
                    i = (k * nz + dz) * nx + dx
                    x_copy(k, dz, dx).wait_recv()
                    total = total + xin[i]
                if dz:
                    acc[k * nz + dz] = total
                    z_copy(k, dz).start()
                else:
                    acc[k * nz] = total
        for k in range(2):
            total = acc[k * nz]
            for dz in range(1, nz):
                z_copy(k, dz).wait_recv()
                total = total + zin[k * nz + dz]
            out_ref[k, rows(s), :] = total
            for copy in plane_targets(k):
                copy.start()
            for copy in own_targets(k):
                copy.start()

    @pl.when(jnp.logical_and(relay, jnp.logical_not(newest)))
    def _():
        for k in range(2):
            arrived(k, s)
            for copy in own_targets(k):
                copy.start()

    @pl.when(relay)
    def _():
        for k in range(2):
            for dz in range(1, nz):
                arrived(k, at(dz, 0))
                for copy in z_targets(k, dz):
                    copy.start()
            for dz in order:
                for dx in range(1, nx):
                    arrived(k, at(dz, dx))
                    for copy in x_targets(k, dz, dx):
                        copy.start()
        for k in range(2):
            for copy in own_targets(k):
                copy.wait_send()
            for dz in range(1, nz):
                for copy in z_targets(k, dz):
                    copy.wait_send()
            for dz in range(nz):
                for dx in range(1, nx):
                    for copy in x_targets(k, dz, dx):
                        copy.wait_send()

    @pl.when(newest)
    def _():
        for k in range(2):
            for copy in plane_targets(k):
                copy.wait_send()
            for dz in order:
                for dx in range(1, nx):
                    x_copy(k, dz, dx).wait_send()
                if dz:
                    z_copy(k, dz).wait_send()

    @pl.when(jnp.logical_not(relay))
    def _():
        for k in range(2):
            for t in range(nspace):
                arrived(k, t)


def gather_rows(partial, nspace, nlag):
    _, gauges, members = partial.shape
    nx = side(nspace)
    nz = nspace // nx
    nc = pad_even(nlag)
    ny = nlag // nc
    chunk = gauges // nspace
    slots = (nx - 1) + (nc - 1) + (nz - 1) + (ny - 1)
    dma = pltpu.SemaphoreType.DMA
    return pl.pallas_call(
        functools.partial(gather_kernel, nspace, nlag),
        out_shape=jax.ShapeDtypeStruct(partial.shape, F32),
        in_specs=[pl.BlockSpec(memory_space=pltpu.VMEM)],
        out_specs=pl.BlockSpec(memory_space=pltpu.VMEM),
        scratch_shapes=[
            pltpu.VMEM((2 * nz, chunk, members), F32),
            pltpu.VMEM((2 * nz * nx, chunk, members), F32),
            pltpu.VMEM((2 * nz, chunk, members), F32),
            dma((2 * nz * nx,)), dma((2 * nz * nx,)),
            dma((2 * nz,)), dma((2 * nz,)),
            dma((2, nspace, slots)), dma((2, nspace)),
        ],
        compiler_params=pltpu.CompilerParams(has_side_effects=True),
    )(partial)


def mm(a, b, tb=False):
    dims = (((1,), (1 if tb else 0,)), ((), ()))
    return lax.dot_general(a, b, dims, preferred_element_type=F32)


def split(a):
    upper = a.astype(BF)
    return upper, (a - upper.astype(F32)).astype(BF)


def mm3(a, b, tb=False):
    (ah, al), (bh, bl) = a, b
    total = mm(ah, bh, tb)
    if bl is not None:
        total = total + mm(ah, bl, tb)
    if al is not None:
        total = total + mm(al, bh, tb)
    return total


def exact(a, b):
    return lax.dot_general(
        a, b, (((1,), (0,)), ((), ())),
        precision=lax.Precision.HIGHEST, preferred_element_type=F32,
    )


def diagonal(shape, start, value):
    row = lax.broadcasted_iota(jnp.int32, shape, 0) + start
    column = lax.broadcasted_iota(jnp.int32, shape, 1)
    return jnp.where(row == column, value, 0.0)


def analysis_kernel(rows_ref, obs_ref, err_ref, ens_ref, out_ref,
                    first, moved, ah, al, ih, il, sh, sl,
                    cov, inv, work, ch, cl, xh, xl, th):
    gauges, members = rows_ref.shape[1:]
    total_rows = ens_ref.shape[0]
    tile = min(256, gauges, total_rows)
    square = (tile, gauges)
    inverse_dof = 1.0 / (members - 1.0)

    def tiles(count, body):
        def step(i, carry):
            body(pl.ds(pl.multiple_of(i * tile, tile), tile), i * tile)
            return carry
        lax.fori_loop(0, count // tile, step, 0)

    def step_of(gap):
        return 2.0 / (2.0 - gap * gap), gap * gap / (2.0 - gap * gap)

    def resplit(at, start):
        xh[at, :], xl[at, :] = split(inv[at, :])

    def wide(gap):
        return gap[0, 0] > 0.1

    def quick(gap):
        factor, gap = step_of(gap)

        def product(at, start):
            th[at, :] = mm(ch[at, :], xh[...]).astype(BF)

        def update(at, start):
            inv[at, :] = factor * (2.0 * inv[at, :] - mm(xh[at, :], th[...]))

        def keep(at, start):
            xh[at, :] = inv[at, :].astype(BF)

        tiles(gauges, product)
        tiles(gauges, update)
        tiles(gauges, keep)
        return gap

    def last(_, carry):
        def product(at, start):
            there = mm3((ch[at, :], cl[at, :]), (xh[...], xl[...]))
            th[at, :] = (diagonal(square, start, 1.0) - there).astype(BF)

        def update(at, start):
            inv[at, :] = inv[at, :] + mm(xh[at, :], th[...])

        tiles(gauges, product)
        tiles(gauges, update)
        tiles(gauges, resplit)
        return carry

    def slow(gap):
        factor, gap = step_of(gap)

        def product(at, start):
            work[0, at, :] = exact(cov[at, :], inv[...])

        def update(at, start):
            x = inv[at, :]
            work[1, at, :] = factor * (2.0 * x - exact(x, work[0]))

        def keep(at, start):
            inv[at, :] = work[1, at, :]

        tiles(gauges, product)
        tiles(gauges, update)
        tiles(gauges, keep)
        return gap

    def invert(k):
        low = jnp.min(err_ref[k], axis=0, keepdims=True)
        sums = jnp.sum(jnp.abs(cov[...]), axis=1, keepdims=True)
        high = jnp.max(sums, axis=0, keepdims=True)
        mid = 2.0 / (low + high)
        factor, gap = step_of((high - low) / (high + low))

        def begin(at, start):
            c = cov[at, :]
            ch[at, :], cl[at, :] = split(c)
            x = (factor * mid) * (diagonal(square, start, 2.0) - mid * c)
            inv[at, :] = x
            xh[at, :] = x.astype(BF)

        tiles(gauges, begin)
        hard = (high - 1000.0 * low)[0, 0] > 0.0

        @pl.when(jnp.logical_not(hard))
        def _():
            lax.while_loop(wide, quick, gap)
            tiles(gauges, resplit)
            lax.fori_loop(0, 2, last, 0)

        @pl.when(hard)
        def _():
            reached = lax.while_loop(wide, slow, gap)
            lax.fori_loop(0, 3, lambda _, g: slow(g), reached)
            tiles(gauges, resplit)

    for k in range(2):
        source = rows_ref.at[0] if k == 0 else moved

        def prepare(at, start):
            r = source[at, :]
            ah[at, :], al[at, :] = split(r - jnp.mean(r, axis=1, keepdims=True))
            ih[at, :], il[at, :] = split(obs_ref[k, at, :] - r)

        def covariance(at, start):
            c = mm3((ah[at, :], al[at, :]), (ah[...], al[...]), True) * inverse_dof
            cov[at, :] = c + diagonal(square, start, err_ref[k, at, :])

        def solve(at, start):
            solved = mm3((xh[at, :], xl[at, :]), (ih[...], il[...]))
            sh[at, :], sl[at, :] = split(solved * inverse_dof)

        def updated(halves):
            part = mm3(halves, (ah[...], al[...]), True)
            return mm3(split(part), (sh[...], sl[...]))

        def move(at, start):
            r = rows_ref[1, at, :]
            moved[at, :] = r + updated((r.astype(BF), None))

        def advance(at, start):
            e = ens_ref[at, :]
            first[at, :] = e.astype(F32) + updated((e, None))

        def finish(at, start):
            f = first[at, :]
            out_ref[at, :] = (f + updated(split(f))).astype(BF)

        tiles(gauges, prepare)
        tiles(gauges, covariance)
        invert(k)
        tiles(gauges, solve)
        if k == 0:
            tiles(gauges, move)
            tiles(total_rows, advance)
        else:
            tiles(total_rows, finish)


def analyse(rows, observed, obs_error, flat):
    _, gauges, members = rows.shape
    total_rows = flat.shape[0]
    return pl.pallas_call(
        analysis_kernel,
        out_shape=jax.ShapeDtypeStruct(flat.shape, BF),
        in_specs=[pl.BlockSpec(memory_space=pltpu.VMEM)] * 4,
        out_specs=pl.BlockSpec(memory_space=pltpu.VMEM),
        scratch_shapes=[
            pltpu.VMEM((total_rows, members), F32),
            pltpu.VMEM((gauges, members), F32),
        ] + [pltpu.VMEM((gauges, members), BF)] * 6 + [
            pltpu.VMEM((gauges, gauges), F32),
            pltpu.VMEM((gauges, gauges), F32),
            pltpu.VMEM((2, gauges, gauges), F32),
        ] + [pltpu.VMEM((gauges, gauges), BF)] * 5,
        compiler_params=pltpu.CompilerParams(vmem_limit_bytes=56 * 1024 * 1024),
    )(rows, observed, obs_error[:, :, None], flat)


def per_device(nspace, nlag, ensemble, observed, obs_error, gauge_rows):
    lag_dev, rows_dev, members = ensemble.shape
    picks = gauge_rows.reshape(-1)
    offset = lax.axis_index("space") * rows_dev
    column = lax.broadcasted_iota(jnp.int32, (picks.shape[0], rows_dev), 1)
    selector = (picks[:, None] - offset == column).astype(BF)
    partial = jnp.dot(selector, ensemble[lag_dev - 1], preferred_element_type=F32)
    rows = gather_rows(partial.reshape(gauge_rows.shape + (members,)), nspace, nlag)
    flat = ensemble.reshape(lag_dev * rows_dev, members)
    return analyse(rows, observed, obs_error, flat).reshape(ensemble.shape)


def solution(mesh):
    in_specs = (P("lag", "space", None), P(), P(), P())
    out_specs = P("lag", "space", None)
    body = functools.partial(per_device, mesh.shape["space"], mesh.shape["lag"])
    return jax.shard_map(
        body, mesh=mesh, in_specs=in_specs, out_specs=out_specs, check_vma=False
    )
```

```python
import functools

import jax
import jax.numpy as jnp
from jax import lax
from jax.experimental import pallas as pl
from jax.experimental.pallas import tpu as pltpu
from jax.sharding import PartitionSpec as P

BF = jnp.bfloat16
F32 = jnp.float32
MESH = pl.DeviceIdType.MESH
TILE = 512
BIG = 1024


def pad_even(n):
    return 2 if n % 2 == 0 else 1


def side(n):
    best = 1
    for inner in range(1, n + 1):
        if n % inner == 0 and inner * inner <= n:
            best = inner
    return best


def gather_kernel(nspace, nlag, p_ref, out_ref, acc, xin, zin, xs, xr, zs, zr, ys, ar):
    nx = side(nspace)
    nz = nspace // nx
    nc = pad_even(nlag)
    ny = nlag // nc
    chunk = p_ref.shape[1] // nspace
    s = lax.axis_index("space")
    l = lax.axis_index("lag")
    z, x = s // nx, s % nx
    y, core = l // nc, l % nc
    newest = l == nlag - 1
    relay = core == nc - 1

    def rows(t):
        return pl.ds(pl.multiple_of(t * chunk, chunk), chunk)

    def at(dz, dx):
        return lax.rem(z + dz, nz) * nx + lax.rem(x + dx, nx)

    def send(src, dst, send_sem, recv_sem, space, lag):
        return pltpu.make_async_remote_copy(
            src_ref=src, dst_ref=dst, send_sem=send_sem, recv_sem=recv_sem,
            device_id=(space, lag), device_id_type=MESH,
        )

    order = list(range(1, nz)) + [0]

    def x_copy(k, dz, dx):
        t = at(dz, dx)
        i = (k * nz + dz) * nx + dx
        return send(p_ref.at[k, rows(t)], xin.at[i], xs.at[i], xr.at[i], at(0, dx), l)

    def z_copy(k, dz):
        i = k * nz + dz
        return send(acc.at[i], zin.at[i], zs.at[i], zr.at[i], at(dz, 0), l)

    def out_copy(k, t, slot, space, lag):
        return send(
            out_ref.at[k, rows(t)], out_ref.at[k, rows(t)],
            ys.at[k, t, slot], ar.at[k, t], space, lag,
        )

    def arrived(k, t):
        pltpu.make_async_copy(
            out_ref.at[k, rows(t)], out_ref.at[k, rows(t)], ar.at[k, t]
        ).wait()

    base_c = nx - 1
    base_z = base_c + (nc - 1)
    base_y = base_z + (nz - 1)

    def own_targets(k):
        copies = [out_copy(k, s, base_z + dz - 1, at(dz, 0), l) for dz in range(nz - 1, 0, -1)]
        copies += [out_copy(k, s, dx - 1, at(0, dx), l) for dx in range(1, nx)]
        copies += [out_copy(k, s, base_c + c, s, y * nc + c) for c in range(nc - 1)]
        return copies

    def plane_targets(k):
        return [out_copy(k, s, base_y + p, s, p * nc + nc - 1) for p in range(ny - 1)]

    def z_targets(k, dz):
        t = at(dz, 0)
        copies = [out_copy(k, t, dx - 1, at(0, dx), l) for dx in range(1, nx)]
        return copies + [out_copy(k, t, base_c + c, s, y * nc + c) for c in range(nc - 1)]

    def x_targets(k, dz, dx):
        t = at(dz, dx)
        return [out_copy(k, t, base_c + c, s, y * nc + c) for c in range(nc - 1)]

    @pl.when(newest)
    def _():
        for k in range(2):
            for dz in order:
                for dx in range(1, nx):
                    x_copy(k, dz, dx).start()
        for k in range(2):
            for dz in order:
                total = p_ref[k, rows(at(dz, 0)), :]
                for dx in range(1, nx):
                    i = (k * nz + dz) * nx + dx
                    x_copy(k, dz, dx).wait_recv()
                    total = total + xin[i]
                if dz:
                    acc[k * nz + dz] = total
                    z_copy(k, dz).start()
                else:
                    acc[k * nz] = total
        for k in range(2):
            total = acc[k * nz]
            for dz in range(1, nz):
                z_copy(k, dz).wait_recv()
                total = total + zin[k * nz + dz]
            out_ref[k, rows(s), :] = total
            for copy in plane_targets(k):
                copy.start()
            for copy in own_targets(k):
                copy.start()

    @pl.when(jnp.logical_and(relay, jnp.logical_not(newest)))
    def _():
        for k in range(2):
            arrived(k, s)
            for copy in own_targets(k):
                copy.start()

    @pl.when(relay)
    def _():
        for k in range(2):
            for dz in range(1, nz):
                arrived(k, at(dz, 0))
                for copy in z_targets(k, dz):
                    copy.start()
            for dz in order:
                for dx in range(1, nx):
                    arrived(k, at(dz, dx))
                    for copy in x_targets(k, dz, dx):
                        copy.start()
        for k in range(2):
            for copy in own_targets(k):
                copy.wait_send()
            for dz in range(1, nz):
                for copy in z_targets(k, dz):
                    copy.wait_send()
            for dz in range(nz):
                for dx in range(1, nx):
                    for copy in x_targets(k, dz, dx):
                        copy.wait_send()

    @pl.when(newest)
    def _():
        for k in range(2):
            for copy in plane_targets(k):
                copy.wait_send()
            for dz in order:
                for dx in range(1, nx):
                    x_copy(k, dz, dx).wait_send()
                if dz:
                    z_copy(k, dz).wait_send()

    @pl.when(jnp.logical_not(relay))
    def _():
        for k in range(2):
            for t in range(nspace):
                arrived(k, t)


def gather_rows(partial, nspace, nlag):
    _, gauges, members = partial.shape
    nx = side(nspace)
    nz = nspace // nx
    nc = pad_even(nlag)
    ny = nlag // nc
    chunk = gauges // nspace
    slots = (nx - 1) + (nc - 1) + (nz - 1) + (ny - 1)
    dma = pltpu.SemaphoreType.DMA
    return pl.pallas_call(
        functools.partial(gather_kernel, nspace, nlag),
        out_shape=jax.ShapeDtypeStruct(partial.shape, F32),
        in_specs=[pl.BlockSpec(memory_space=pltpu.VMEM)],
        out_specs=pl.BlockSpec(memory_space=pltpu.VMEM),
        scratch_shapes=[
            pltpu.VMEM((2 * nz, chunk, members), F32),
            pltpu.VMEM((2 * nz * nx, chunk, members), F32),
            pltpu.VMEM((2 * nz, chunk, members), F32),
            dma((2 * nz * nx,)), dma((2 * nz * nx,)),
            dma((2 * nz,)), dma((2 * nz,)),
            dma((2, nspace, slots)), dma((2, nspace)),
        ],
        compiler_params=pltpu.CompilerParams(has_side_effects=True),
    )(partial)


def mm(a, b, tb=False):
    dims = (((1,), (1 if tb else 0,)), ((), ()))
    return lax.dot_general(a, b, dims, preferred_element_type=F32)


def split(a):
    upper = a.astype(BF)
    return upper, (a - upper.astype(F32)).astype(BF)


def exact(a, b):
    return lax.dot_general(
        a, b, (((1,), (0,)), ((), ())),
        precision=lax.Precision.HIGHEST, preferred_element_type=F32,
    )


def diagonal(shape, start, value):
    row = lax.broadcasted_iota(jnp.int32, shape, 0) + start
    column = lax.broadcasted_iota(jnp.int32, shape, 1)
    return jnp.where(row == column, value, 0.0)


def analysis_kernel(rows_ref, obs_ref, err_ref, ens_ref, out_ref,
                    first, moved, acat, icat, scat,
                    cov, inv, work, ch, cl, xcat, th):
    gauges, members = rows_ref.shape[1:]
    total_rows = ens_ref.shape[0]
    tile = min(TILE, gauges, total_rows)
    big = min(BIG, total_rows)
    square = (tile, gauges)
    inverse_dof = 1.0 / (members - 1.0)

    def tiles(count, body, tile=tile):
        def step(i, carry):
            body(pl.ds(pl.multiple_of(i * tile, tile), tile), i * tile)
            return carry
        if count == tile:
            body(pl.ds(0, tile), 0)
        else:
            lax.fori_loop(0, count // tile, step, 0)

    def below(ref, at, start, halves):
        upper, lower = halves
        ref[pl.ds(start, tile), :] = upper
        ref[pl.ds(start + gauges, tile), :] = lower
        ref[pl.ds(start + 2 * gauges, tile), :] = upper

    def beside(halves):
        upper, lower = halves
        return jnp.concatenate([upper, upper, lower], axis=1)

    def step_of(gap):
        return 2.0 / (2.0 - gap * gap), gap * gap / (2.0 - gap * gap)

    def resplit(at, start):
        below(xcat, at, start, split(inv[at, :]))

    def is_wide(gap):
        return gap[0, 0] > 0.1

    def quick(gap):
        factor, gap = step_of(gap)

        def product(at, start):
            th[at, :] = mm(ch[at, :], xcat[:gauges, :]).astype(BF)

        def update(at, start):
            inv[at, :] = factor * (2.0 * inv[at, :] - mm(xcat[at, :], th[...]))

        def keep(at, start):
            xcat[at, :] = inv[at, :].astype(BF)

        tiles(gauges, product)
        tiles(gauges, update)
        tiles(gauges, keep)
        return gap

    def last(_, carry):
        def product(at, start):
            there = mm(beside((ch[at, :], cl[at, :])), xcat[...])
            th[at, :] = (diagonal(square, start, 1.0) - there).astype(BF)

        def update(at, start):
            inv[at, :] = inv[at, :] + mm(xcat[at, :], th[...])

        tiles(gauges, product)
        tiles(gauges, update)
        tiles(gauges, resplit)
        return carry

    def slow(gap):
        factor, gap = step_of(gap)

        def product(at, start):
            work[0, at, :] = exact(cov[at, :], inv[...])

        def update(at, start):
            x = inv[at, :]
            work[1, at, :] = factor * (2.0 * x - exact(x, work[0]))

        def keep(at, start):
            inv[at, :] = work[1, at, :]

        tiles(gauges, product)
        tiles(gauges, update)
        tiles(gauges, keep)
        return gap

    def invert(k):
        low = jnp.min(err_ref[k], axis=0, keepdims=True)
        sums = jnp.sum(jnp.abs(cov[...]), axis=1, keepdims=True)
        high = jnp.max(sums, axis=0, keepdims=True)
        mid = 2.0 / (low + high)
        factor, gap = step_of((high - low) / (high + low))

        def begin(at, start):
            c = cov[at, :]
            ch[at, :], cl[at, :] = split(c)
            x = (factor * mid) * (diagonal(square, start, 2.0) - mid * c)
            inv[at, :] = x
            xcat[at, :] = x.astype(BF)

        tiles(gauges, begin)
        hard = (high - 1000.0 * low)[0, 0] > 0.0

        @pl.when(jnp.logical_not(hard))
        def _():
            lax.while_loop(is_wide, quick, gap)
            tiles(gauges, resplit)
            lax.fori_loop(0, 2, last, 0)

        @pl.when(hard)
        def _():
            reached = lax.while_loop(is_wide, slow, gap)
            lax.fori_loop(0, 3, lambda _, g: slow(g), reached)
            tiles(gauges, resplit)

    for k in range(2):
        source = rows_ref.at[0] if k == 0 else moved

        def prepare(at, start):
            r = source[at, :]
            upper, lower = split(r - jnp.mean(r, axis=1, keepdims=True))
            acat[at, :] = jnp.concatenate([upper, lower, upper], axis=1)
            below(icat, at, start, split(obs_ref[k, at, :] - r))

        def covariance(at, start):
            left = beside((acat[at, :members], acat[at, members:2 * members]))
            c = mm(left, acat[...], True) * inverse_dof
            cov[at, :] = c + diagonal(square, start, err_ref[k, at, :])

        def solve(at, start):
            left = beside((xcat[at, :], xcat[pl.ds(start + gauges, tile), :]))
            below(scat, at, start, split(mm(left, icat[...]) * inverse_dof))

        def updated(left):
            part = mm(left, acat[:, :left.shape[1]], True)
            return mm(beside(split(part)), scat[...])

        def twice(e):
            return jnp.concatenate([e, e], axis=1)

        def move(at, start):
            r = rows_ref[1, at, :]
            moved[at, :] = r + updated(twice(r.astype(BF)))

        def advance(at, start):
            e = ens_ref[at, :]
            first[at, :] = e.astype(F32) + updated(twice(e))

        def finish(at, start):
            f = first[at, :]
            out_ref[at, :] = (f + updated(beside(split(f)))).astype(BF)

        tiles(gauges, prepare)
        tiles(gauges, covariance)
        invert(k)
        tiles(gauges, solve)
        if k == 0:
            tiles(gauges, move)
            tiles(total_rows, advance, big)
        else:
            tiles(total_rows, finish, big)


def analyse(rows, observed, obs_error, flat):
    _, gauges, members = rows.shape
    total_rows = flat.shape[0]
    return pl.pallas_call(
        analysis_kernel,
        out_shape=jax.ShapeDtypeStruct(flat.shape, BF),
        in_specs=[pl.BlockSpec(memory_space=pltpu.VMEM)] * 4,
        out_specs=pl.BlockSpec(memory_space=pltpu.VMEM),
        scratch_shapes=[
            pltpu.VMEM((total_rows, members), F32),
            pltpu.VMEM((gauges, members), F32),
            pltpu.VMEM((gauges, 3 * members), BF),
            pltpu.VMEM((3 * gauges, members), BF),
            pltpu.VMEM((3 * gauges, members), BF),
            pltpu.VMEM((gauges, gauges), F32),
            pltpu.VMEM((gauges, gauges), F32),
            pltpu.VMEM((2, gauges, gauges), F32),
            pltpu.VMEM((gauges, gauges), BF),
            pltpu.VMEM((gauges, gauges), BF),
            pltpu.VMEM((3 * gauges, gauges), BF),
            pltpu.VMEM((gauges, gauges), BF),
        ],
        compiler_params=pltpu.CompilerParams(vmem_limit_bytes=56 * 1024 * 1024),
    )(rows, observed, obs_error[:, :, None], flat)


def per_device(nspace, nlag, ensemble, observed, obs_error, gauge_rows):
    lag_dev, rows_dev, members = ensemble.shape
    picks = gauge_rows.reshape(-1)
    offset = lax.axis_index("space") * rows_dev
    column = lax.broadcasted_iota(jnp.int32, (picks.shape[0], rows_dev), 1)
    selector = (picks[:, None] - offset == column).astype(BF)
    partial = jnp.dot(selector, ensemble[lag_dev - 1], preferred_element_type=F32)
    rows = gather_rows(partial.reshape(gauge_rows.shape + (members,)), nspace, nlag)
    flat = ensemble.reshape(lag_dev * rows_dev, members)
    return analyse(rows, observed, obs_error, flat).reshape(ensemble.shape)


def solution(mesh):
    in_specs = (P("lag", "space", None), P(), P(), P())
    out_specs = P("lag", "space", None)
    body = functools.partial(per_device, mesh.shape["space"], mesh.shape["lag"])
    return jax.shard_map(
        body, mesh=mesh, in_specs=in_specs, out_specs=out_specs, check_vma=False
    )
```
